512 devices in a mesh: lat: 16 (over y, x_hi), lon: 32 (over z, x_lo, core).
Axes of the slice: x: 4 (x_hi: 2, x_lo: 2; x = x_hi * 2 + x_lo), y: 8, z: 8, core: 2. Of those that a mesh axis runs over, the one named last changes fastest.
Arguments:
- tokens: bfloat16 [2, 192, 768, 512], P(None, 'lat', 'lon'), may hold values from -6 to 6
- level_ids: int32 [2, 192, 768], P(None, 'lat', 'lon'), may hold values from 0 to 2
- coarse_ids: int32 [2, 96, 384], P(None, 'lat', 'lon'), may hold values from 0 to 2
- first_qkv: bfloat16 [512, 1536], replicated, may hold values from -1.25 to 1.25
- first_out: bfloat16 [512, 512], replicated, may hold values from -0.25 to 0.25
- merge_weight: bfloat16 [2048, 1024], P('lon'), may hold values from -0.125 to 0.125
- second_qkv: bfloat16 [1024, 3072], P('lon'), may hold values from -1.25 to 1.25
- second_out: bfloat16 [1024, 1024], P('lon'), may hold values from -0.1875 to 0.1875
Outputs:
- skip: bfloat16 [2, 192, 768, 512], P(None, 'lat', 'lon')
- coarse: bfloat16 [2, 96, 384, 1024], P(None, 'lat', 'lon')
The draws below stay inside these ranges and needn't reach their ends.
All inputs are finite; a program needn't handle non-finite values.
Results may differ from the reference program's by a relative error of at most 0.012.
Values may be sent and summed in bfloat16 or wider, within the bound.
A program may use at most 64 MiB of HBM per device.

```python
import math
import jax
import jax.numpy as jnp
from jax import lax

D1 = 512
D2 = 1024
HEADS1 = 8
HEADS2 = 16
WIN_LEVELS = 2
WIN_ROWS = 6
WIN_COLS = 12
LEVELS = 2
NLAT = 192
NLON = 768


def projection_draw(key, width):
    base = jax.random.truncated_normal(key, -4.0, 4.0, (width, 3 * width), jnp.float32) / jnp.sqrt(jnp.float32(width))
    base = jnp.clip(base, -1.25, 1.25)
    return base.astype(jnp.bfloat16)


def draw_first_qkv(key, part):
    return projection_draw(jax.random.fold_in(key, 11), D1)


def draw_second_qkv(key, part):
    return projection_draw(jax.random.fold_in(key, 13), D2)


def plant(values, key, low, high):
    index_at = [jax.random.randint(jax.random.fold_in(key, axis), (), 0, length) for axis, length in enumerate(values.shape)]
    main_axis = values.shape.index(max(values.shape))
    beside = index_at[:main_axis] + [(index_at[main_axis] + 1) % values.shape[main_axis]] + index_at[main_axis + 1:]
    return values.at[tuple(index_at)].set(low).at[tuple(beside)].set(high)


def block_levels(key, extent, cuts, low, top_value):
    loudness, own = 1.0, jax.random.fold_in(key, 6)
    for axis_at, blocks in cuts:
        heights = jnp.exp(jax.random.uniform(jax.random.fold_in(own, axis_at), (blocks,), jnp.float32, low / len(cuts), top_value / len(cuts)))
        loudness = loudness * jnp.repeat(heights, extent[axis_at] // blocks).reshape([-1 if axis == axis_at else 1 for axis in range(len(extent))])
    return loudness


def centred(stream_key, extent, scale, reach, split=(), dtype=jnp.bfloat16):
    drawn = scale * jax.random.normal(stream_key, extent, jnp.float32)
    if split:
        drawn = drawn * block_levels(stream_key, extent, split, -0.22, 0.18)
    return jnp.clip(drawn, -reach, reach).astype(dtype)


def setup_inputs(seed: int = 0) -> dict:
    splits = jax.random.split(jax.random.key(seed), 9)
    return {
        "tokens": centred(splits[0], (LEVELS, NLAT, NLON, D1), 1.0, 6.0, ((1, 16), (2, 32))),
        "level_ids": plant(jax.random.randint(splits[1], (LEVELS, NLAT, NLON), 0, 3), jax.random.fold_in(splits[1], 1), 0, 2).astype(jnp.int32),
        "coarse_ids": plant(jax.random.randint(splits[2], (LEVELS, NLAT // 2, NLON // 2), 0, 3), jax.random.fold_in(splits[2], 1), 0, 2).astype(jnp.int32),
        "first_qkv": draw_first_qkv(jax.random.fold_in(splits[8], 71), 0),
        "first_out": centred(splits[4], (D1, D1), D1 ** -0.5, 0.25),
        "merge_weight": centred(splits[5], (4 * D1, D2), (4 * D1) ** -0.5, 0.125, ((0, 32),)),
        "second_qkv": draw_second_qkv(jax.random.fold_in(splits[8], 71), 0),
        "second_out": centred(splits[7], (D2, D2), D2 ** -0.5, 0.1875, ((0, 32),)),
    }


EPSILON = 1e-05

def normalized(values):
    widened = values.astype(jnp.float32)
    center = lax.optimization_barrier(jnp.mean(widened, axis=-1, keepdims=True))
    spread = lax.optimization_barrier(jnp.mean(jnp.square(widened - center), axis=-1, keepdims=True))
    return ((widened - center) * lax.rsqrt(spread + EPSILON)).astype(jnp.bfloat16)

def window_softmax(queries, keys, values, labels, heads):
    levels, rows, columns, width = queries.shape
    stacks = levels // WIN_LEVELS
    across = columns // WIN_COLS
    head_size = width // heads

    def windows(array):
        shaped = array.reshape(stacks, WIN_LEVELS, rows, across, WIN_COLS, heads, head_size)
        shaped = shaped.transpose(0, 3, 1, 2, 4, 5, 6)
        return shaped.reshape(stacks * across, WIN_LEVELS * rows * WIN_COLS, heads, head_size).astype(jnp.float32)
    marks = labels.reshape(stacks, WIN_LEVELS, rows, across, WIN_COLS).transpose(0, 3, 1, 2, 4)
    marks = marks.reshape(stacks * across, WIN_LEVELS * rows * WIN_COLS)
    scores = jnp.einsum('wqhd,wkhd->whqk', windows(queries), windows(keys)) / math.sqrt(head_size)
    allowed = marks[:, None, :, None] == marks[:, None, None, :]
    scores = jnp.where(allowed, scores, -1e+30)
    highest = lax.optimization_barrier(jnp.max(scores, axis=-1, keepdims=True))
    expos = jnp.exp(scores - highest)
    weights = (expos / lax.optimization_barrier(jnp.sum(expos, axis=-1, keepdims=True))).astype(jnp.bfloat16)
    mixed = jnp.einsum('whqk,wkhd->wqhd', weights.astype(jnp.float32), windows(values)).astype(jnp.bfloat16)
    mixed = mixed.reshape(stacks, across, WIN_LEVELS, rows, WIN_COLS, width).transpose(0, 2, 3, 1, 4, 5)
    return mixed.reshape(levels, rows, columns, width)

def shifted_layer(field, labels, qkv_weight, out_weight, heads):
    half_rows = WIN_ROWS // 2
    half_cols = WIN_COLS // 2
    levels, height, breadth, width = field.shape
    moved = jnp.roll(field, (-half_rows, -half_cols), (1, 2))
    marks = jnp.roll(labels, (-half_rows, -half_cols), (1, 2))
    bands = height // WIN_ROWS

    def by_band(array):
        return jnp.moveaxis(array.reshape((levels, bands, WIN_ROWS) + array.shape[2:]), 1, 0)

    def one_band(pair):
        band, band_marks = pair
        normed = normalized(band).reshape(-1, width)
        packed = jnp.dot(normed, qkv_weight, preferred_element_type=jnp.float32).astype(jnp.bfloat16)
        packed = packed.reshape(levels, WIN_ROWS, breadth, 3 * width)
        mixed = window_softmax(packed[..., :width], packed[..., width:2 * width], packed[..., 2 * width:], band_marks, heads)
        update = jnp.dot(mixed.reshape(-1, width), out_weight, preferred_element_type=jnp.float32).reshape(band.shape)
        return (band.astype(jnp.float32) + update).astype(jnp.bfloat16)
    result = lax.map(one_band, (by_band(moved), by_band(marks)))
    result = jnp.moveaxis(result, 0, 1).reshape(field.shape)
    return jnp.roll(result, (half_rows, half_cols), (1, 2))

def edge_labels(ids):
    height = ids.shape[1]
    edge = (jnp.arange(height) < WIN_ROWS // 2).astype(jnp.int32)
    return ids * 2 + edge[None, :, None]

def merge_patches(field):
    levels, height, breadth, width = field.shape
    shaped = field.reshape(levels, height // 2, 2, breadth // 2, 2, width).transpose(0, 1, 3, 4, 2, 5)
    return shaped.reshape(levels, height // 2, breadth // 2, 4 * width)

def reference(tokens, level_ids, coarse_ids, first_qkv, first_out, merge_weight, second_qkv, second_out):
    skip = shifted_layer(tokens, edge_labels(level_ids), first_qkv, first_out, HEADS1)
    joined = merge_patches(skip)
    levels, height, breadth, width = joined.shape
    merged = jnp.dot(normalized(joined).reshape(-1, width), merge_weight, preferred_element_type=jnp.float32)
    merged = merged.astype(jnp.bfloat16).reshape(levels, height, breadth, merge_weight.shape[1])
    coarse = shifted_layer(merged, edge_labels(coarse_ids), second_qkv, second_out, HEADS2)
    return (skip, coarse)
```

```python
import functools

import jax
import jax.numpy as jnp
import numpy as np
from jax import lax
from jax.experimental import pallas as pl
from jax.experimental.pallas import tpu as pltpu
from jax.sharding import PartitionSpec as P

EPSILON = 1e-05
QUAD = 40
TOKENS = 4 * QUAD
GROUP = 4
HEAD = 64
MESH = pl.DeviceIdType.MESH
F32 = jnp.float32
BF16 = jnp.bfloat16


def one_hot_tables():
    pick = np.zeros((2, TOKENS, 288), np.float32)
    merge = np.zeros((TOKENS, TOKENS), np.float32)
    expand = np.zeros((144, TOKENS), np.float32)
    expand2 = np.zeros((96, 2 * QUAD), np.float32)
    tile = np.zeros((TOKENS, GROUP * TOKENS), np.float32)
    marks = np.zeros((TOKENS, 4 * 192), np.float32)
    for level in range(2):
        for r in range(3):
            for c in range(6):
                at = level * 18 + r * 6 + c
                for q in range(4):
                    rh, ch = divmod(q, 2)
                    row = q * QUAD + at
                    for w in range(2):
                        col = level * 144 + (rh * 3 + r) * 24 + 6 + 4 * w + ch * 6 + c
                        pick[w, row, col] = 1
                    fr, fc = 2 * r + q % 2, 2 * c + q // 2
                    sub = (fr // 3) * 2 + fc // 6
                    merge[row, sub * QUAD + level * 18 + (fr % 3) * 6 + fc % 6] = 1
                    expand[level * 72 + r * 24 + q * 6 + c, row] = 1
                    source = rh * 2 + ch
                    r_in, c_in = (r + 3 if rh == 0 else r), (c + 6 if ch == 0 else c)
                    marks[row, source * 192 + level * 96 + r_in * 16 + c_in] = 1
                for q in range(2):
                    expand2[(level * 3 + r) * 16 + q * 6 + c, q * QUAD + at] = 1
    for h in range(GROUP):
        tile[np.arange(TOKENS), h * TOKENS + np.arange(TOKENS)] = 1
    return [t.astype(BF16) for t in (pick, merge, expand, expand2, tile, marks)]


def dot(a, b, dims=((1,), (0,))):
    return lax.dot_general(a, b, (dims, ((), ())), preferred_element_type=F32)


def normalized(x):
    center = jnp.mean(x, axis=-1, keepdims=True)
    x = x - center
    spread = jnp.mean(x * x, axis=-1, keepdims=True)
    return (x * lax.rsqrt(spread + EPSILON)).astype(BF16)


def score_bias(marks, tile):
    across = dot(marks, tile, ((0,), (0,)))
    keys = marks.astype(F32)[:, :1]
    return jnp.where(keys == across[:1, :], 0.0, -1e30).astype(F32)


def attend(q, k, v, bias):
    lane = lax.broadcasted_iota(jnp.int32, (TOKENS, GROUP * HEAD), 1)
    scaled = q * BF16(0.125)
    zero = jnp.zeros_like(q)
    stacked = jnp.concatenate(
        [jnp.where(lane // HEAD == h, scaled, zero) for h in range(GROUP)], axis=0
    )
    scores = dot(k, stacked, ((1,), (1,))) + bias
    expos = jnp.exp(scores - jnp.max(scores, axis=0, keepdims=True)).astype(BF16)
    extended = jnp.concatenate([v, jnp.ones((TOKENS, 128), BF16)], axis=1)
    both = dot(expos, extended, ((0,), (0,)))
    part = lambda h: both[h * TOKENS : (h + 1) * TOKENS]
    halves = []
    for pair in range(2):
        first, second = part(2 * pair), part(2 * pair + 1)
        low = lane[:, :128] < HEAD
        at = slice(pair * 128, pair * 128 + 128)
        top = jnp.where(low, first[:, at], second[:, at])
        total = jnp.where(low, first[:, 256:], second[:, 256:])
        halves.append(top / total)
    return jnp.concatenate(halves, axis=1)


def kernel(
    sizes,
    tokens, lab1, lab2, first_qkv, first_out, merge_weight, second_qkv, second_out,
    pick, merge, expand, expand2, tile, marks,
    skip_out, coarse_out,
    X, L1, L2, WQ1, WO1, GW, PK, MX, OUTQ, FINE, SKQ, SK, MG, JN, PK2, MX2, COQ, CQ, CO,
    local_sem, halo_recv, mid_recv, skip_recv, back_recv, send_sem, gather_sem, sib_sem, drain_sem, out_sem,
):
    nlat, nlon = sizes
    lat, lon = lax.axis_index("lat"), lax.axis_index("lon")
    up, down = lax.rem(lat + nlat - 1, nlat), lax.rem(lat + 1, nlat)
    left, right = lax.rem(lon + nlon - 1, nlon), lax.rem(lon + 1, nlon)
    nz = nlon // 4
    z = lon // 4
    core = lax.rem(lon, 2)
    x_lo = lax.rem(lon // 2, 2)
    sibling = lon + 1 - 2 * core
    across = lon + 2 - 4 * x_lo
    other_lat = lat + 1 - 2 * lax.rem(lat, 2)
    z_next, z_prev = lax.rem(lon + 4, nlon), lax.rem(lon + nlon - 4, nlon)

    def local(src, dst, n):
        copy = pltpu.make_async_copy(src, dst, local_sem.at[n])
        copy.start()
        return copy

    own = [local(merge_weight, GW.at[lon, 0:64], 0)]
    for n in range(3):
        own.append(
            local(second_qkv.at[:, n * 1024 : (n + 1) * 1024], GW.at[lon, 64 + 32 * n : 96 + 32 * n], 1 + n)
        )
    own.append(local(second_out, GW.at[lon, 160:192], 4))
    mine = [
        local(tokens, X.at[:, 0:12, 0:24], 5),
        local(lab1, L1.at[:, 0:12, 0:24], 6),
        local(lab2, L2.at[0], 7),
        local(first_qkv, WQ1, 8),
        local(first_out, WO1, 9),
    ]

    barrier = pltpu.get_barrier_semaphore()
    partners = [
        (up, lon), (down, lon), (lat, left), (lat, right), (up, left), (down, right),
        (lat, z_next), (lat, z_prev), (lat, across), (other_lat, across), (lat, sibling),
    ]
    for partner in partners:
        pl.semaphore_signal(barrier, inc=1, device_id=partner, device_id_type=MESH)
    pl.semaphore_wait(barrier, len(partners))

    sends = []

    def send(src, dst, recv, to):
        copy = pltpu.make_async_remote_copy(
            src_ref=src, dst_ref=dst, send_sem=send_sem.at[len(sends)], recv_sem=recv,
            device_id=to, device_id_type=MESH,
        )
        copy.start()
        sends.append(copy)

    corners = [
        ((lat, left), slice(0, 12), slice(0, 8), slice(0, 12), slice(24, 32)),
        ((up, lon), slice(0, 3), slice(0, 24), slice(12, 15), slice(0, 24)),
        ((up, left), slice(0, 3), slice(0, 8), slice(12, 15), slice(24, 32)),
    ]
    for n, (to, r, c, r_to, c_to) in enumerate(corners):
        send(tokens.at[:, r, c], X.at[:, r_to, c_to], halo_recv.at[3 * n], to)
        send(lab1.at[:, r, c], L1.at[:, r_to, c_to], halo_recv.at[3 * n + 1], to)
        send(lab2, L2.at[n + 1], halo_recv.at[3 * n + 2], to)

    def await_halo(n):
        to, r, c, r_to, c_to = corners[n]
        for src, dst, s in (
            (tokens.at[:, r, c], X.at[:, r_to, c_to], 0),
            (lab1.at[:, r, c], L1.at[:, r_to, c_to], 1),
            (lab2, L2.at[n + 1], 2),
        ):
            pltpu.make_async_copy(dst, dst, halo_recv.at[3 * n + s]).wait()

    def piece(c, shard, first=0, rows=64):
        return GW.at[shard, 64 * c + first : 64 * c + first + rows]

    def forward(c, shard, to, recv, first=0, rows=64):
        ref = piece(c, shard, first, rows)
        pltpu.make_async_remote_copy(
            src_ref=ref, dst_ref=ref, send_sem=drain_sem.at[c], recv_sem=recv,
            device_id=to, device_id_type=MESH,
        ).start()

    def shard_at(step):
        return lax.rem(lon + 4 * step + nlon, nlon)

    def across_shard(shard):
        return shard + 2 - 4 * lax.rem(shard // 2, 2)

    def spread(c, shard):
        hop = lax.rem(shard // 4, 2)
        forward(c, shard, (lat + hop * (other_lat - lat), across), gather_sem.at[c, shard])
        forward(c, shard, (lat, sibling), sib_sem.at[c])

    def arrived(c, shard):
        ref = piece(c, shard)
        pltpu.make_async_copy(ref, ref, gather_sem.at[c, shard]).wait()

    half = nz // 2

    def gather_step(c, k):
        if k == 0:
            forward(c, lon, (lat, z_next), gather_sem.at[c, lon])
            forward(c, lon, (lat, z_prev), gather_sem.at[c, lon])
            spread(c, lon)
        elif k < half:
            behind, ahead = shard_at(-k), shard_at(k)
            arrived(c, behind)
            first = dict(first=0, rows=32) if k == half - 1 else {}
            forward(c, behind, (lat, z_next), gather_sem.at[c, behind], **first)
            arrived(c, ahead)
            second = dict(first=32, rows=32) if k == half - 1 else {}
            forward(c, ahead, (lat, z_prev), gather_sem.at[c, ahead], **second)
            spread(c, behind)
            spread(c, ahead)
        elif k == half:
            arrived(c, shard_at(half))
            spread(c, shard_at(half))
        k = k - 1
        if k >= 0:
            for step in sorted({k, -k} if k < half else {half}):
                shard = across_shard(shard_at(step))
                arrived(c, shard)
                forward(c, shard, (lat, sibling), sib_sem.at[c])

    def await_weights(c):
        ref = GW.at[0 : nlon // 2, 64 * c : 64 * c + 64]
        pltpu.make_async_copy(ref, ref, sib_sem.at[c]).wait()

    for copy in own:
        copy.wait()
    pending = []
    for c in range(3):
        pending += [(c, k) for k in range(half + 2)]
    order = [(0, 0), (1, 0)] + [(0, 1), (1, 1), (0, 2), (1, 2), (0, 3), (1, 3), (0, 4), (1, 4), (2, 0), (0, 5)]
    order += [(1, 5), (2, 1), (2, 2), (2, 3), (2, 4), (2, 5)]
    assert sorted(order) == sorted(pending)

    def service(n):
        for _ in range(n):
            if order:
                gather_step(*order.pop(0))

    service(2)
    for copy in mine:
        copy.wait()

    def spot(a, b):
        return ((a // 2) * 2 + b // 2) * 4 + (a % 2) * 2 + b % 2

    def window(b, w):
        r_at, c_at = slice(3 + 6 * b, 9 + 6 * b), slice(8 * w, 8 * w + 24)
        field = X[:, r_at, c_at].reshape(288, 512)
        labels = L1[:, r_at, c_at].reshape(288, 128)
        select = pick[w]
        rolled = dot(select, field)
        bias = score_bias(dot(select, labels).astype(BF16), tile[...])
        normed = normalized(rolled)
        for n in range(3):
            PK[:, 512 * n : 512 * n + 512] = dot(normed, WQ1[:, 512 * n : 512 * n + 512]).astype(BF16)
        for g in range(2):
            at = 256 * g
            mixed = attend(
                PK[:, at : at + 256], PK[:, 512 + at : 768 + at], PK[:, 1024 + at : 1280 + at], bias
            )
            MX[:, at : at + 256] = mixed.astype(BF16)
            if g == 0:
                service(1)
        update = rolled + dot(MX[...], WO1[...])
        for q in range(4):
            r, c = 2 * b + q // 2, 2 * w + q % 2
            value = update[q * QUAD : (q + 1) * QUAD].astype(BF16)
            OUTQ[4 * r + c] = value
            if r >= 1 and c >= 1:
                FINE[spot(r - 1, c - 1)] = value
            if r <= 2 and c <= 2:
                SKQ[4 * (r + 1) + c + 1] = value
        service(1)
        for q in range(4):
            r, c = 2 * b + q // 2, 2 * w + q % 2
            if r == 0 or c == 0:
                to = (lat if r else up, lon if c else left)
                at = spot(r - 1 if r else 3, c - 1 if c else 3)
                send(OUTQ.at[4 * r + c], FINE.at[at], mid_recv.at[at], to)
            if r == 3 or c == 3:
                to = (down if r == 3 else lat, right if c == 3 else lon)
                at = 4 * ((r + 1) % 4) + (c + 1) % 4
                send(OUTQ.at[4 * r + c], SKQ.at[at], skip_recv.at[at], to)

    window(0, 0)
    await_halo(0)
    window(0, 1)
    await_halo(1)
    window(1, 0)
    await_halo(2)
    window(1, 1)

    def rows(ref, at):
        return jnp.concatenate([ref[n].astype(F32) for n in at], axis=0).astype(BF16)

    for at in [0, 1, 2, 3, 4, 8, 12]:
        pltpu.make_async_copy(SKQ.at[at], SKQ.at[at], skip_recv.at[at]).wait()
    for r in range(4):
        block = dot(expand[...], rows(SKQ, range(4 * r, 4 * r + 4)))
        SK[:, 3 * r : 3 * r + 3] = block.reshape(2, 3, 24, 512).astype(BF16)
    skip_copy = pltpu.make_async_copy(SK, skip_out, out_sem.at[0])
    skip_copy.start()
    service(4)

    for a, b in [(0, 3), (1, 3), (2, 3), (3, 0), (3, 1), (3, 2), (3, 3)]:
        at = spot(a, b)
        pltpu.make_async_copy(FINE.at[at], FINE.at[at], mid_recv.at[at]).wait()
    joined = []
    for q in range(4):
        parts = dot(merge[...], rows(FINE, range(4 * q, 4 * q + 4)))
        joined.append(jnp.concatenate([parts[p * QUAD : (p + 1) * QUAD] for p in range(4)], axis=1))
    JN[...] = normalized(jnp.concatenate(joined, axis=0))
    bias = score_bias(dot(marks[...], L2[...].reshape(768, 128)).astype(BF16), tile[...])
    service(1)
    while order and order[0][0] < 2:
        service(1)
    await_weights(0)

    def merge_part(n, carry):
        at = pl.ds(pl.multiple_of(n * 256, 256), 256)
        weight = GW[:, 0:64, at].reshape(nlon * 64, 256)
        MG[:, at] = dot(JN[...], weight)
        return carry

    lax.fori_loop(0, 4, merge_part, 0)
    merged = MG[...].astype(BF16).astype(F32)
    JN[:, 0:1024] = normalized(merged)
    while order:
        service(1)
    await_weights(1)
    await_weights(2)

    def qkv_part(n, carry):
        row = pl.ds(pl.multiple_of(64 + 32 * (n // 4), 32), 32)
        at = pl.ds(pl.multiple_of(lax.rem(n, 4) * 256, 256), 256)
        weight = GW[:, row, at].reshape(nlon * 32, 256)
        PK2[n] = dot(JN[:, 0:1024], weight).astype(BF16)
        return carry

    lax.fori_loop(0, 12, qkv_part, 0)

    def heads_part(g, carry):
        MX2[g] = attend(PK2[g], PK2[4 + g], PK2[8 + g], bias).astype(BF16)
        return carry

    lax.fori_loop(0, 4, heads_part, 0)
    mixed = jnp.concatenate([MX2[g] for g in range(4)], axis=1)
    JN[:, 1024:2048] = mixed

    def out_part(n, carry):
        at = pl.ds(pl.multiple_of(n * 256, 256), 256)
        weight = GW[:, 160:192, at].reshape(nlon * 32, 256)
        result = MG[:, at].astype(BF16).astype(F32) + dot(JN[:, 1024:2048], weight)
        for q in range(4):
            COQ[q, :, at] = result[q * QUAD : (q + 1) * QUAD].astype(BF16)
        return carry

    lax.fori_loop(0, 4, out_part, 0)

    CQ[3] = COQ[0]
    send(COQ.at[1], CQ.at[2], back_recv.at[2], (lat, right))
    send(COQ.at[2], CQ.at[1], back_recv.at[1], (down, lon))
    send(COQ.at[3], CQ.at[0], back_recv.at[0], (down, right))
    for at in range(3):
        pltpu.make_async_copy(CQ.at[at], CQ.at[at], back_recv.at[at]).wait()
    for r in range(2):
        block = dot(expand2[...], rows(CQ, (2 * r, 2 * r + 1))).reshape(2, 3, 16, 1024)
        CO[:, 3 * r : 3 * r + 3] = block[:, :, 0:12].astype(BF16)
    coarse_copy = pltpu.make_async_copy(CO, coarse_out, out_sem.at[1])
    coarse_copy.start()
    skip_copy.wait()
    coarse_copy.wait()
    for copy in sends:
        copy.wait_send()
    for c in range(3):
        ref = GW.at[0 : nlon - 1, 0:64]
        pltpu.make_async_copy(ref, ref, drain_sem.at[c]).wait()


def edge_labels(ids):
    height = ids.shape[1]
    global_rows = lax.axis_index("lat") * height + jnp.arange(height)
    edge = (global_rows < 3).astype(jnp.int32)
    return ids * 2 + edge[None, :, None] + 1


def per_device(
    sizes,
    tokens, level_ids, coarse_ids, first_qkv, first_out, merge_weight, second_qkv, second_out,
):
    nlat, nlon = sizes
    spread = lambda a: jnp.broadcast_to(a.astype(BF16)[..., None], a.shape + (128,))
    lab1 = spread(edge_labels(level_ids))
    lab2 = spread(jnp.pad(edge_labels(coarse_ids), ((0, 0), (0, 0), (0, 4))))
    tables = [jnp.asarray(t) for t in one_hot_tables()]
    anywhere = pl.BlockSpec(memory_space=pl.ANY)
    vmem = pl.BlockSpec(memory_space=pltpu.VMEM)
    scratch = [
        pltpu.VMEM((2, 15, 32, 512), BF16),
        pltpu.VMEM((2, 15, 32, 128), BF16),
        pltpu.VMEM((4, 2, 6, 16, 128), BF16),
        pltpu.VMEM((512, 1536), BF16),
        pltpu.VMEM((512, 512), BF16),
        pltpu.VMEM((nlon, 192, 1024), BF16),
        pltpu.VMEM((TOKENS, 1536), BF16),
        pltpu.VMEM((TOKENS, 512), BF16),
        pltpu.VMEM((16, QUAD, 512), BF16),
        pltpu.VMEM((16, QUAD, 512), BF16),
        pltpu.VMEM((16, QUAD, 512), BF16),
        pltpu.VMEM((2, 12, 24, 512), BF16),
        pltpu.VMEM((TOKENS, 1024), F32),
        pltpu.VMEM((TOKENS, 2048), BF16),
        pltpu.VMEM((12, TOKENS, 256), BF16),
        pltpu.VMEM((4, TOKENS, 256), BF16),
        pltpu.VMEM((4, QUAD, 1024), BF16),
        pltpu.VMEM((4, QUAD, 1024), BF16),
        pltpu.VMEM((2, 6, 12, 1024), BF16),
        pltpu.SemaphoreType.DMA((10,)),
        pltpu.SemaphoreType.DMA((9,)),
        pltpu.SemaphoreType.DMA((16,)),
        pltpu.SemaphoreType.DMA((16,)),
        pltpu.SemaphoreType.DMA((3,)),
        pltpu.SemaphoreType.DMA((26,)),
        pltpu.SemaphoreType.DMA((3, nlon)),
        pltpu.SemaphoreType.DMA((3,)),
        pltpu.SemaphoreType.DMA((3,)),
        pltpu.SemaphoreType.DMA((2,)),
    ]
    return pl.pallas_call(
        functools.partial(kernel, sizes),
        out_shape=(
            jax.ShapeDtypeStruct(tokens.shape, BF16),
            jax.ShapeDtypeStruct(coarse_ids.shape + (1024,), BF16),
        ),
        in_specs=[anywhere] * 8 + [vmem] * 6,
        out_specs=(anywhere, anywhere),
        scratch_shapes=scratch,
        compiler_params=pltpu.CompilerParams(
            collective_id=0, has_side_effects=True, vmem_limit_bytes=56 * 1024 * 1024
        ),
        name="swin",
    )(
        tokens, lab1, lab2, first_qkv, first_out, merge_weight, second_qkv, second_out, *tables
    )


def solution(mesh):
    placed = (
        P(None, "lat", "lon", None),
        P(None, "lat", "lon"),
        P(None, "lat", "lon"),
        P(),
        P(),
        P("lon", None),
        P("lon", None),
        P("lon", None),
    )
    return jax.shard_map(
        functools.partial(per_device, (mesh.shape["lat"], mesh.shape["lon"])),
        mesh=mesh,
        in_specs=placed,
        out_specs=(P(None, "lat", "lon", None), P(None, "lat", "lon", None)),
        check_vma=False,
    )
```
